32 devices in a mesh: parts: 2 (over x), gx: 4 (over y, core), gy: 4 (over z).
Axes of the slice: x: 2, y: 2, z: 4, core: 2. Of those that a mesh axis runs over, the one named last changes fastest.
Arguments:
- forcing_right_side: float32 [32, 32, 1024], P(('parts', 'gx'), 'gy'), parts along dimension 0, may hold values from -18 to 18
- earlier_warmth: float32 [32, 32, 1024], P(('parts', 'gx'), 'gy'), parts along dimension 0, may hold values from 0 to 2
- matter_condition: int32 [32, 32, 1024], P(('parts', 'gx'), 'gy'), parts along dimension 0, may hold values from 0 to 2
- compressed_slot_number: int32 [32, 32, 1024], P(('parts', 'gx'), 'gy'), parts along dimension 0, may hold values from 0 to 127
- normal_draw_factor: float32 [32, 32, 1024], P(('parts', 'gx'), 'gy'), parts along dimension 0, may hold values from -6 to 6
Outputs:
- solution: float32 [32, 32, 1024], P(('parts', 'gx'), 'gy'), parts along dimension 0
- residual: float32 [32, 32, 1024], P(('parts', 'gx'), 'gy'), parts along dimension 0
The draws below stay inside these ranges and needn't reach their ends.
There are 2 independent parts, one for each index of `parts`. The reference program is written for one: setup_inputs(seed, part) draws one part's arguments, and reference() takes and returns one part's arrays. A program takes and returns all parts, laid end to end along the dimension named above; each array names one. Nothing has to cross between parts.
Inputs may be any that keep to these rules, and one draw needn't show every extreme that they name: `matter_condition`: phase labels the cell as powder, solid or liquid. `compressed_slot_number`: each cell's row of the sketch.
All inputs are finite; a program needn't handle non-finite values.
Results may differ from the reference program's by a relative error of at most 0.0003.
Values sent between devices are 32-bit elements; how exact they have to be, the bound alone decides.
A program may use at most 64 MiB of HBM per device.

```python
import jax
import jax.numpy as jnp
from jax import lax

MESH_SPAN_UPWARD = 1024
BASIS = 2
CYCLES = 1
SKETCH = 128
MESH_SPAN_EAST = 16
MESH_SPAN_NORTH = 32


def set_ends(entries, rng, low, largest):
    place = [jax.random.randint(jax.random.fold_in(rng, axis), (), 0, length) for axis, length in enumerate(entries.shape)]
    widest = entries.shape.index(max(entries.shape))
    next_to = place[:widest] + [(place[widest] + 1) % entries.shape[widest]] + place[widest + 1:]
    return entries.at[tuple(place)].set(low).at[tuple(next_to)].set(largest)


def steps_of(key, dims, shards, low, top_value):
    factor_of, own = 1.0, jax.random.fold_in(key, 6)
    for axis_at, blocks in shards:
        steps = jnp.exp(jax.random.uniform(jax.random.fold_in(own, axis_at), (blocks,), jnp.float32, low / len(shards), top_value / len(shards)))
        factor_of = factor_of * jnp.repeat(steps, dims[axis_at] // blocks).reshape([-1 if axis == axis_at else 1 for axis in range(len(dims))])
    return factor_of


def gaussian(rng, dims, spread, limit, shards=(), kind=jnp.bfloat16):
    factor_of = steps_of(rng, dims, shards, -0.22, 0.18) if shards else 1.0
    entries = jax.random.normal(rng, dims, jnp.float32) * spread * factor_of
    return jnp.minimum(jnp.maximum(entries, -limit), limit).astype(kind)


def setup_inputs(seed: int = 0, part: int = 0) -> dict:
    key_list = jax.random.split(jax.random.key(seed), 6)
    part_splits = jax.random.split(jax.random.fold_in(key_list[5], part), 6)
    forcing_right_side = gaussian(part_splits[0], (MESH_SPAN_EAST, MESH_SPAN_NORTH, MESH_SPAN_UPWARD), 3.0, 18.0, ((0, 4), (1, 4)), jnp.float32)
    earlier_warmth = jnp.clip(2.0 * jax.random.uniform(part_splits[1], (MESH_SPAN_EAST, MESH_SPAN_NORTH, MESH_SPAN_UPWARD), jnp.float32) ** steps_of(part_splits[1], (MESH_SPAN_EAST, MESH_SPAN_NORTH, MESH_SPAN_UPWARD), ((0, 4), (1, 4)), -0.2, 0.2), 0.0, 2.0)
    matter_condition = set_ends(jax.random.randint(part_splits[2], (MESH_SPAN_EAST, MESH_SPAN_NORTH, MESH_SPAN_UPWARD), 0, 3), jax.random.fold_in(part_splits[2], 1), 0, 2).astype(jnp.int32)
    compressed_slot_number = set_ends(jax.random.randint(part_splits[3], (MESH_SPAN_EAST, MESH_SPAN_NORTH, MESH_SPAN_UPWARD), 0, SKETCH), jax.random.fold_in(part_splits[3], 1), 0, SKETCH - 1).astype(jnp.int32)
    normal_draw_factor = gaussian(part_splits[4], (MESH_SPAN_EAST, MESH_SPAN_NORTH, MESH_SPAN_UPWARD), 1.0, 6.0, ((0, 4), (1, 4)), jnp.float32)
    return {"forcing_right_side": forcing_right_side, "earlier_warmth": earlier_warmth, "matter_condition": matter_condition, "compressed_slot_number": compressed_slot_number, "normal_draw_factor": normal_draw_factor}


epsilon = 1e-06
highest = lax.Precision.HIGHEST

def medium_traits(earlier_warmth, matter_condition):
    datum_offset = jnp.where(matter_condition == 0, 0.2, jnp.where(matter_condition == 1, 1.0, 0.6)).astype(jnp.float32)
    spreading_rate = datum_offset * (0.5 + earlier_warmth)
    volumetric_retention = jnp.where(matter_condition == 0, 1.0, jnp.where(matter_condition == 1, 2.0, 1.5)).astype(jnp.float32)
    return (spreading_rate, volumetric_retention)

def harmonic(first, second):
    return 2.0 * first * second / (first + second)

def shifted(field):
    padded = jnp.pad(field, 1)
    return [padded[2:, 1:-1, 1:-1], padded[:-2, 1:-1, 1:-1], padded[1:-1, 2:, 1:-1], padded[1:-1, :-2, 1:-1], padded[1:-1, 1:-1, 2:], padded[1:-1, 1:-1, :-2]]

def operate(field, volumetric_retention, links):
    result = volumetric_retention * field
    for conductance, neighbour in zip(links, shifted(field)):
        result = result + conductance * (field - neighbour)
    return result

def solve_small(hess, scale_norm):
    width_count = hess.shape[1]
    gram_matrix = jnp.dot(hess.T, hess, precision=highest)
    target = scale_norm * hess[0]
    factor = jnp.linalg.cholesky(gram_matrix)
    forward = []
    for row_a in range(width_count):
        partial_sum = target[row_a]
        for prior in range(row_a):
            partial_sum = partial_sum - factor[row_a, prior] * forward[prior]
        forward.append(partial_sum / factor[row_a, row_a])
    backward = [None] * width_count
    for row_a in reversed(range(width_count)):
        partial_sum = forward[row_a]
        for later in range(row_a + 1, width_count):
            partial_sum = partial_sum - factor[later, row_a] * backward[later]
        backward[row_a] = partial_sum / factor[row_a, row_a]
    return backward

def reference(forcing_right_side, earlier_warmth, matter_condition, compressed_slot_number, normal_draw_factor):
    spreading_rate, volumetric_retention = medium_traits(earlier_warmth, matter_condition)
    links = [harmonic(spreading_rate, other) for other in shifted(spreading_rate)]

    def sketch_of(field):
        return jax.ops.segment_sum((normal_draw_factor * field).reshape(-1), compressed_slot_number.reshape(-1), num_segments=SKETCH)
    solution = jnp.zeros_like(forcing_right_side)
    residual = forcing_right_side
    for cycle_number in range(CYCLES):
        if cycle_number > 0:
            residual = forcing_right_side - operate(solution, volumetric_retention, links)
        sketched = sketch_of(residual)
        scale_norm = jnp.sqrt(jnp.sum(sketched * sketched) + epsilon)
        basis_list = [residual / scale_norm]
        sketch_list = [sketched / scale_norm]
        columns = []
        for column in range(BASIS):
            images = operate(basis_list[column], volumetric_retention, links)
            image_sketch = sketch_of(images)
            stacked = jnp.stack(sketch_list, axis=1)
            coeffs = jnp.dot(stacked.T, image_sketch, precision=highest)
            reduced = images
            for prior in range(column + 1):
                reduced = reduced - coeffs[prior] * basis_list[prior]
            remainder = sketch_of(reduced)
            norm_next = jnp.sqrt(jnp.sum(remainder * remainder) + epsilon)
            columns.append(jnp.concatenate([coeffs, norm_next[None], jnp.zeros((BASIS - column - 1,), coeffs.dtype)]))
            if column + 1 < BASIS:
                basis_list.append(reduced / norm_next)
                sketch_list.append(remainder / norm_next)
        hess = jnp.stack(columns, axis=1)
        weights = solve_small(hess, scale_norm)
        for prior in range(BASIS):
            solution = solution + weights[prior] * basis_list[prior]
    residual = forcing_right_side - operate(solution, volumetric_retention, links)
    return (solution, residual)
```

```python
import functools

import jax
import jax.numpy as jnp
from jax import lax
from jax.experimental import pallas as pl
from jax.experimental.pallas import tpu as pltpu
from jax.sharding import PartitionSpec as P

SKETCH = 128
LOW = 16
HIGH = SKETCH // LOW
MESH = pl.DeviceIdType.MESH
epsilon = 1e-06
highest = lax.Precision.HIGHEST
f32 = jnp.float32
bf16 = jnp.bfloat16


def harmonic(first, second):
    return 2.0 * first * second / (first + second)


def total(field):
    return jnp.sum(jnp.sum(field, axis=1, keepdims=True), axis=0, keepdims=True)


def coefficients(s0, s1, s2):
    beta = jnp.sqrt(total(s0 * s0) + epsilon)
    inv_beta = 1.0 / beta
    q0 = s0 * inv_beta
    p0 = s1 * inv_beta
    h00 = total(q0 * p0)
    t0 = p0 - h00 * q0
    n0 = jnp.sqrt(total(t0 * t0) + epsilon)
    inv_n0 = 1.0 / n0
    q1 = t0 * inv_n0
    p1 = (s2 * inv_beta - h00 * p0) * inv_n0
    h01 = total(q0 * p1)
    h11 = total(q1 * p1)
    t1 = p1 - h01 * q0 - h11 * q1
    n1sq = total(t1 * t1) + epsilon
    m00 = h00 * h00 + n0 * n0
    m01 = h00 * h01 + n0 * h11
    m11 = h01 * h01 + h11 * h11 + n1sq
    b0 = beta * h00
    b1 = beta * h01
    l00 = jnp.sqrt(m00)
    l10 = m01 / l00
    l11 = jnp.sqrt(m11 - l10 * l10)
    f0 = b0 / l00
    f1 = (b1 - l10 * f0) / l11
    y1 = f1 / l11
    y0 = (f0 - l10 * y1) / l00
    c1 = y1 * inv_beta * inv_n0
    c0 = y0 * inv_beta - c1 * h00
    return c0, c1


def kernel(
    ngx, ngy, nx, ny, nz,
    f_hbm, w_hbm, m_hbm, s_hbm, d_hbm,
    z1, z2, c_out,
    r, w, m, slot, d, cond, cap, lx, ly, lylow, lz, onehot, wh, wl,
    hx_r, hx_c, hx_z, hy_rc, hy_z, py_rc, py_z,
    mine, gathered, load_sem, hs_sem, hr_sem, as_sem, ar_sem,
):
    gx = lax.axis_index("gx")
    gy = lax.axis_index("gy")
    count = ngx * ngy
    me = gx * ngy + gy

    loads = [
        pltpu.make_async_copy(src, dst, load_sem.at[i])
        for i, (src, dst) in enumerate(
            ((w_hbm, w), (m_hbm, m), (f_hbm, r), (s_hbm, slot), (d_hbm, d))
        )
    ]
    for load in loads:
        load.start()

    def peer(step):
        other = lax.rem(me + step, count)
        return {"gx": lax.div(other, ngy), "gy": lax.rem(other, ngy)}

    barrier = pltpu.get_barrier_semaphore()

    def greet(step, carry):
        pl.semaphore_signal(barrier, inc=1, device_id=peer(step), device_id_type=MESH)
        return carry

    lax.fori_loop(1, count, greet, 0)

    has_x = (gx > 0, gx < ngx - 1)
    has_y = (gy > 0, gy < ngy - 1)
    to_x = ({"gx": gx - 1, "gy": gy}, {"gx": gx + 1, "gy": gy})
    to_y = ({"gx": gx, "gy": gy - 1}, {"gx": gx, "gy": gy + 1})
    edge_x = (0, nx - 1)
    edge_y = (0, ny - 1)

    def remote(src, dst, index, side, target):
        return pltpu.make_async_remote_copy(
            src_ref=src,
            dst_ref=dst.at[1 - side],
            send_sem=hs_sem.at[index, side],
            recv_sem=hr_sem.at[index, 1 - side],
            device_id=target,
            device_id_type=MESH,
        )

    def x_copies(src, dst, index):
        return [(has_x[s], remote(src.at[edge_x[s]], dst, index, s, to_x[s])) for s in (0, 1)]

    def y_copies(src, dst, index):
        return [(has_y[s], remote(src.at[s], dst, index, s, to_y[s])) for s in (0, 1)]

    def begin(copies):
        for there, copy in copies:
            pl.when(there)(copy.start)

    def arrive(copies):
        for there, copy in copies:
            pl.when(there)(copy.wait_send)

    def recv_wait(dst, index, side, src, there, target):
        copy = pltpu.make_async_remote_copy(
            src_ref=src,
            dst_ref=dst.at[side],
            send_sem=hs_sem.at[index, side],
            recv_sem=hr_sem.at[index, side],
            device_id=target,
            device_id_type=MESH,
        )
        pl.when(there)(copy.wait_recv)

    loads[0].wait()
    loads[1].wait()
    for x in range(nx):
        phase = m[x]
        cond[x] = jnp.where(phase == 0, 0.2, jnp.where(phase == 1, 1.0, 0.6)).astype(f32) * (0.5 + w[x])
        cap[x] = jnp.where(phase == 0, 1.0, jnp.where(phase == 1, 2.0, 1.5)).astype(f32)
    loads[2].wait()
    for s in (0, 1):
        for x in range(nx):
            py_rc[s, pl.ds(x, 1), :] = r[x, pl.ds(edge_y[s], 1), :]
            py_rc[s, pl.ds(nx + x, 1), :] = cond[x, pl.ds(edge_y[s], 1), :]

        @pl.when(jnp.logical_not(has_x[s]))
        def _():
            hx_r[s] = jnp.zeros((ny, nz), f32)
            hx_c[s] = jnp.zeros((ny, nz), f32)
            hx_z[s] = jnp.zeros((ny, nz), f32)

        @pl.when(jnp.logical_not(has_y[s]))
        def _():
            hy_rc[s] = jnp.zeros((2 * nx, nz), f32)
            hy_z[s] = jnp.zeros((nx, nz), f32)

    pl.semaphore_wait(barrier, count - 1)
    first = x_copies(cond, hx_c, 0) + y_copies(py_rc, hy_rc, 1) + x_copies(r, hx_r, 2)
    begin(first)

    lane = lax.broadcasted_iota(jnp.int32, (ny, nz), 1)
    row = lax.broadcasted_iota(jnp.int32, (ny, nz), 0)
    row_high = lax.broadcasted_iota(jnp.int32, (HIGH, nz), 0)
    row_low = lax.broadcasted_iota(jnp.int32, (LOW, nz), 0)

    def spread(x_ref, x, y, rows):
        return jnp.broadcast_to(x_ref[x, pl.ds(y, 1), :], (rows, nz))

    for x in range(nx):
        here = cond[x]
        if x > 0:
            lx[x] = harmonic(cond[x - 1], here)
        lz[x] = jnp.where(lane == nz - 1, 0.0, harmonic(here, pltpu.roll(here, nz - 1, 1)))
    loads[3].wait()
    loads[4].wait()

    def build(x, carry):
        for y in range(ny):
            low = jnp.bitwise_and(spread(slot, x, y, LOW), LOW - 1)
            onehot[x, y] = jnp.where(low == row_low, 1.0, 0.0).astype(bf16)
        return carry

    lax.fori_loop(0, nx, build, 0)

    def sketch(field):
        for x in range(nx):
            weighted = d[x] * field[x]
            upper = weighted.astype(bf16).astype(f32)
            wh[x] = upper
            wl[x] = weighted - upper

        def add(x, sums):
            for y in range(ny):
                mask = lax.shift_right_logical(spread(slot, x, y, HIGH), 4) == row_high
                left = jnp.concatenate(
                    [
                        jnp.where(mask, spread(wh, x, y, HIGH), 0.0),
                        jnp.where(mask, spread(wl, x, y, HIGH), 0.0),
                    ],
                    axis=0,
                ).astype(bf16)
                sums = sums + lax.dot_general(
                    left, onehot[x, y], (((1,), (1,)), ((), ())), preferred_element_type=f32
                )
            return sums

        sums = lax.fori_loop(0, nx, add, jnp.zeros((2 * HIGH, LOW), f32))
        both = sums[:HIGH] + sums[HIGH:]
        lanes = lax.broadcasted_iota(jnp.int32, (LOW, SKETCH), 1)
        expand = jnp.where(
            jnp.bitwise_and(lanes, LOW - 1) == lax.broadcasted_iota(jnp.int32, (LOW, SKETCH), 0), 1.0, 0.0
        ).astype(f32)
        wide = jnp.dot(both, expand, precision=highest, preferred_element_type=f32)
        keep = lax.shift_right_logical(
            lax.broadcasted_iota(jnp.int32, (HIGH, SKETCH), 1), 4
        ) == lax.broadcasted_iota(jnp.int32, (HIGH, SKETCH), 0)
        return jnp.sum(jnp.where(keep, wide, 0.0), axis=0, keepdims=True)

    def apply(field, halo_x, halo_y, out):
        for x in range(nx):
            v = field[x]
            below = halo_x[0] if x == 0 else field[x - 1]
            above = halo_x[1] if x == nx - 1 else field[x + 1]
            acc = cap[x] * v + lx[x + 1] * (v - above) + lx[x] * (v - below)
            up = jnp.where(row == ny - 1, halo_y(1, x), pltpu.roll(v, ny - 1, 0))
            flux = ly[x] * (v - up)
            entering = lylow[pl.ds(x, 1), :] * (halo_y(0, x) - v[0:1, :])
            acc = acc + flux - jnp.where(row == 0, entering, pltpu.roll(flux, 1, 0))
            flux = lz[x] * (v - pltpu.roll(v, nz - 1, 1))
            out[x] = acc + flux - pltpu.roll(flux, 1, 1)

    mine[3:4, :] = jnp.zeros((1, SKETCH), f32)
    mine[0:1, :] = sketch(r)

    for s in (0, 1):
        recv_wait(hx_c, 0, s, cond.at[0], has_x[s], to_x[s])
        recv_wait(hy_rc, 1, s, py_rc.at[0], has_y[s], to_y[s])
        recv_wait(hx_r, 2, s, r.at[0], has_x[s], to_x[s])
    lx[0] = harmonic(hx_c[0], cond[0])
    lx[nx] = harmonic(cond[nx - 1], hx_c[1])
    for x in range(nx):
        here = cond[x]
        up = jnp.where(row == ny - 1, hy_rc[1, pl.ds(nx + x, 1), :], pltpu.roll(here, ny - 1, 0))
        ly[x] = harmonic(here, up)
        lylow[pl.ds(x, 1), :] = harmonic(hy_rc[0, pl.ds(nx + x, 1), :], here[0:1, :])
    apply(r, hx_r, lambda s, x: hy_rc[s, pl.ds(x, 1), :], z1)
    for s in (0, 1):
        for x in range(nx):
            py_z[s, pl.ds(x, 1), :] = z1[x, pl.ds(edge_y[s], 1), :]
    second = x_copies(z1, hx_z, 3) + y_copies(py_z, hy_z, 4)
    begin(second)
    mine[1:2, :] = sketch(z1)
    for s in (0, 1):
        recv_wait(hx_z, 3, s, z1.at[0], has_x[s], to_x[s])
        recv_wait(hy_z, 4, s, py_z.at[0], has_y[s], to_y[s])
    apply(z1, hx_z, lambda s, x: hy_z[s, pl.ds(x, 1), :], z2)
    mine[2:3, :] = sketch(z2)

    def share(step, carry):
        pltpu.make_async_remote_copy(
            src_ref=mine,
            dst_ref=gathered.at[me],
            send_sem=as_sem.at[step],
            recv_sem=ar_sem.at[me],
            device_id=peer(step),
            device_id_type=MESH,
        ).start()
        return carry

    lax.fori_loop(1, count, share, 0)
    gathered[me] = mine[...]
    arrive(first)
    arrive(second)

    def collect(step, carry):
        other = lax.rem(me + step, count)
        copy = pltpu.make_async_remote_copy(
            src_ref=mine,
            dst_ref=gathered.at[other],
            send_sem=as_sem.at[step],
            recv_sem=ar_sem.at[other],
            device_id=peer(step),
            device_id_type=MESH,
        )
        copy.wait_recv()
        copy.wait_send()
        return carry

    lax.fori_loop(1, count, collect, 0)
    summed = jnp.sum(gathered[...], axis=0)
    c0, c1 = coefficients(summed[0:1], summed[1:2], summed[2:3])
    c_out[0:1, :] = jnp.broadcast_to(c0, (1, SKETCH))
    c_out[1:2, :] = jnp.broadcast_to(c1, (1, SKETCH))


def body(ngx, ngy, f, w, m, s, d):
    nx, ny, nz = f.shape
    count = ngx * ngy
    vm = lambda shape, dtype=f32: pltpu.VMEM(shape, dtype)
    block = (nx, ny, nz)
    z1, z2, c = pl.pallas_call(
        functools.partial(kernel, ngx, ngy, nx, ny, nz),
        out_shape=(
            jax.ShapeDtypeStruct(block, f32),
            jax.ShapeDtypeStruct(block, f32),
            jax.ShapeDtypeStruct((2, SKETCH), f32),
        ),
        in_specs=[pl.BlockSpec(memory_space=pl.ANY)] * 5,
        out_specs=[pl.BlockSpec(memory_space=pltpu.VMEM)] * 3,
        scratch_shapes=[
            vm(block), vm(block), vm(block, jnp.int32), vm(block, jnp.int32), vm(block),
            vm(block), vm(block),
            vm((nx + 1, ny, nz)), vm(block), vm((nx, nz)), vm(block),
            vm((nx, ny, LOW, nz), bf16), vm(block), vm(block),
            vm((2, ny, nz)), vm((2, ny, nz)), vm((2, ny, nz)),
            vm((2, 2 * nx, nz)), vm((2, nx, nz)),
            vm((2, 2 * nx, nz)), vm((2, nx, nz)),
            vm((4, SKETCH)), vm((count, 4, SKETCH)),
            pltpu.SemaphoreType.DMA((5,)),
            pltpu.SemaphoreType.DMA((5, 2)),
            pltpu.SemaphoreType.DMA((5, 2)),
            pltpu.SemaphoreType.DMA((count,)),
            pltpu.SemaphoreType.DMA((count,)),
        ],
        compiler_params=pltpu.CompilerParams(collective_id=0, has_side_effects=True),
        name="sketched_gmres",
    )(f, w, m, s, d)
    c0 = c[0, 0]
    c1 = c[1, 0]
    return c0 * f + c1 * z1, f - c0 * z1 - c1 * z2


def solution(mesh):
    spec = P(("parts", "gx"), "gy", None)
    return jax.shard_map(
        functools.partial(body, mesh.shape["gx"], mesh.shape["gy"]),
        mesh=mesh,
        in_specs=(spec,) * 5,
        out_specs=(spec, spec),
        check_vma=False,
    )
```

```python
import functools

import jax
import jax.numpy as jnp
from jax import lax
from jax.experimental import pallas as pl
from jax.experimental.pallas import tpu as pltpu
from jax.sharding import PartitionSpec as P

SKETCH = 128
LOW = 16
HIGH = SKETCH // LOW
MESH = pl.DeviceIdType.MESH
epsilon = 1e-06
highest = lax.Precision.HIGHEST
f32 = jnp.float32
bf16 = jnp.bfloat16


def harmonic(first, second):
    return 2.0 * first * second / (first + second)


def total(field):
    return jnp.sum(jnp.sum(field, axis=1, keepdims=True), axis=0, keepdims=True)


def coefficients(s0, s1, s2):
    beta = jnp.sqrt(total(s0 * s0) + epsilon)
    inv_beta = 1.0 / beta
    q0 = s0 * inv_beta
    p0 = s1 * inv_beta
    h00 = total(q0 * p0)
    t0 = p0 - h00 * q0
    n0 = jnp.sqrt(total(t0 * t0) + epsilon)
    inv_n0 = 1.0 / n0
    q1 = t0 * inv_n0
    p1 = (s2 * inv_beta - h00 * p0) * inv_n0
    h01 = total(q0 * p1)
    h11 = total(q1 * p1)
    t1 = p1 - h01 * q0 - h11 * q1
    n1sq = total(t1 * t1) + epsilon
    m00 = h00 * h00 + n0 * n0
    m01 = h00 * h01 + n0 * h11
    m11 = h01 * h01 + h11 * h11 + n1sq
    b0 = beta * h00
    b1 = beta * h01
    l00 = jnp.sqrt(m00)
    l10 = m01 / l00
    l11 = jnp.sqrt(m11 - l10 * l10)
    f0 = b0 / l00
    f1 = (b1 - l10 * f0) / l11
    y1 = f1 / l11
    y0 = (f0 - l10 * y1) / l00
    c1 = y1 * inv_beta * inv_n0
    c0 = y0 * inv_beta - c1 * h00
    return c0, c1


def kernel(
    ngx, ngy, nx, ny, nz,
    f_hbm, w_hbm, m_hbm, s_hbm, d_hbm,
    answer, rest,
    z1, z2, r, w, m, slot, d, cond, cap, lx, ly, lylow, lz, onehot, wh, wl,
    hx_r, hx_c, hx_z, hy_rc, hy_z, py_rc, py_z,
    mine, gathered, load_sem, hs_sem, hr_sem, as_sem, ar_sem,
):
    gx = lax.axis_index("gx")
    gy = lax.axis_index("gy")
    count = ngx * ngy
    me = gx * ngy + gy

    loads = [
        pltpu.make_async_copy(src, dst, load_sem.at[i])
        for i, (src, dst) in enumerate(
            ((w_hbm, w), (m_hbm, m), (f_hbm, r), (s_hbm, slot), (d_hbm, d))
        )
    ]
    for load in loads:
        load.start()

    def peer(step):
        other = lax.rem(me + step, count)
        return {"gx": lax.div(other, ngy), "gy": lax.rem(other, ngy)}

    barrier = pltpu.get_barrier_semaphore()

    def greet(step, carry):
        pl.semaphore_signal(barrier, inc=1, device_id=peer(step), device_id_type=MESH)
        return carry

    lax.fori_loop(1, count, greet, 0)

    has_x = (gx > 0, gx < ngx - 1)
    has_y = (gy > 0, gy < ngy - 1)
    to_x = ({"gx": gx - 1, "gy": gy}, {"gx": gx + 1, "gy": gy})
    to_y = ({"gx": gx, "gy": gy - 1}, {"gx": gx, "gy": gy + 1})
    edge_x = (0, nx - 1)
    edge_y = (0, ny - 1)

    def remote(src, dst, index, side, target):
        return pltpu.make_async_remote_copy(
            src_ref=src,
            dst_ref=dst.at[1 - side],
            send_sem=hs_sem.at[index, side],
            recv_sem=hr_sem.at[index, 1 - side],
            device_id=target,
            device_id_type=MESH,
        )

    def x_copies(src, dst, index):
        return [(has_x[s], remote(src.at[edge_x[s]], dst, index, s, to_x[s])) for s in (0, 1)]

    def y_copies(src, dst, index):
        return [(has_y[s], remote(src.at[s], dst, index, s, to_y[s])) for s in (0, 1)]

    def begin(copies):
        for there, copy in copies:
            pl.when(there)(copy.start)

    def arrive(copies):
        for there, copy in copies:
            pl.when(there)(copy.wait_send)

    def recv_wait(dst, index, side, src, there, target):
        copy = pltpu.make_async_remote_copy(
            src_ref=src,
            dst_ref=dst.at[side],
            send_sem=hs_sem.at[index, side],
            recv_sem=hr_sem.at[index, side],
            device_id=target,
            device_id_type=MESH,
        )
        pl.when(there)(copy.wait_recv)

    loads[0].wait()
    loads[1].wait()
    for x in range(nx):
        phase = m[x]
        cond[x] = jnp.where(phase == 0, 0.2, jnp.where(phase == 1, 1.0, 0.6)).astype(f32) * (0.5 + w[x])
        cap[x] = jnp.where(phase == 0, 1.0, jnp.where(phase == 1, 2.0, 1.5)).astype(f32)
    loads[2].wait()
    for s in (0, 1):
        for x in range(nx):
            py_rc[s, pl.ds(x, 1), :] = r[x, pl.ds(edge_y[s], 1), :]
            py_rc[s, pl.ds(nx + x, 1), :] = cond[x, pl.ds(edge_y[s], 1), :]

        @pl.when(jnp.logical_not(has_x[s]))
        def _():
            hx_r[s] = jnp.zeros((ny, nz), f32)
            hx_c[s] = jnp.zeros((ny, nz), f32)
            hx_z[s] = jnp.zeros((ny, nz), f32)

        @pl.when(jnp.logical_not(has_y[s]))
        def _():
            hy_rc[s] = jnp.zeros((2 * nx, nz), f32)
            hy_z[s] = jnp.zeros((nx, nz), f32)

    pl.semaphore_wait(barrier, count - 1)
    first = x_copies(cond, hx_c, 0) + y_copies(py_rc, hy_rc, 1) + x_copies(r, hx_r, 2)
    begin(first)

    lane = lax.broadcasted_iota(jnp.int32, (ny, nz), 1)
    row = lax.broadcasted_iota(jnp.int32, (ny, nz), 0)
    row_high = lax.broadcasted_iota(jnp.int32, (HIGH, nz), 0)
    row_low = lax.broadcasted_iota(jnp.int32, (LOW, nz), 0)

    def spread(x_ref, x, y, rows):
        return jnp.broadcast_to(x_ref[x, pl.ds(y, 1), :], (rows, nz))

    for x in range(nx):
        here = cond[x]
        if x > 0:
            lx[x] = harmonic(cond[x - 1], here)
        lz[x] = jnp.where(lane == nz - 1, 0.0, harmonic(here, pltpu.roll(here, nz - 1, 1)))
    loads[3].wait()
    loads[4].wait()

    def build(x, carry):
        for y in range(ny):
            low = jnp.bitwise_and(spread(slot, x, y, LOW), LOW - 1)
            onehot[x, y] = jnp.where(low == row_low, 1.0, 0.0).astype(bf16)
        return carry

    lax.fori_loop(0, nx, build, 0)

    def sketch(field):
        for x in range(nx):
            weighted = d[x] * field[x]
            upper = weighted.astype(bf16).astype(f32)
            wh[x] = upper
            wl[x] = weighted - upper

        def add(x, sums):
            for y in range(ny):
                mask = lax.shift_right_logical(spread(slot, x, y, HIGH), 4) == row_high
                left = jnp.concatenate(
                    [
                        jnp.where(mask, spread(wh, x, y, HIGH), 0.0),
                        jnp.where(mask, spread(wl, x, y, HIGH), 0.0),
                    ],
                    axis=0,
                ).astype(bf16)
                sums = sums + lax.dot_general(
                    left, onehot[x, y], (((1,), (1,)), ((), ())), preferred_element_type=f32
                )
            return sums

        sums = lax.fori_loop(0, nx, add, jnp.zeros((2 * HIGH, LOW), f32))
        both = sums[:HIGH] + sums[HIGH:]
        lanes = lax.broadcasted_iota(jnp.int32, (LOW, SKETCH), 1)
        expand = jnp.where(
            jnp.bitwise_and(lanes, LOW - 1) == lax.broadcasted_iota(jnp.int32, (LOW, SKETCH), 0), 1.0, 0.0
        ).astype(f32)
        wide = jnp.dot(both, expand, precision=highest, preferred_element_type=f32)
        keep = lax.shift_right_logical(
            lax.broadcasted_iota(jnp.int32, (HIGH, SKETCH), 1), 4
        ) == lax.broadcasted_iota(jnp.int32, (HIGH, SKETCH), 0)
        return jnp.sum(jnp.where(keep, wide, 0.0), axis=0, keepdims=True)

    def apply(field, halo_x, halo_y, out):
        for x in range(nx):
            v = field[x]
            below = halo_x[0] if x == 0 else field[x - 1]
            above = halo_x[1] if x == nx - 1 else field[x + 1]
            acc = cap[x] * v + lx[x + 1] * (v - above) + lx[x] * (v - below)
            up = jnp.where(row == ny - 1, halo_y(1, x), pltpu.roll(v, ny - 1, 0))
            flux = ly[x] * (v - up)
            entering = lylow[pl.ds(x, 1), :] * (halo_y(0, x) - v[0:1, :])
            acc = acc + flux - jnp.where(row == 0, entering, pltpu.roll(flux, 1, 0))
            flux = lz[x] * (v - pltpu.roll(v, nz - 1, 1))
            out[x] = acc + flux - pltpu.roll(flux, 1, 1)

    mine[3:4, :] = jnp.zeros((1, SKETCH), f32)
    mine[0:1, :] = sketch(r)

    for s in (0, 1):
        recv_wait(hx_c, 0, s, cond.at[0], has_x[s], to_x[s])
        recv_wait(hy_rc, 1, s, py_rc.at[0], has_y[s], to_y[s])
        recv_wait(hx_r, 2, s, r.at[0], has_x[s], to_x[s])
    lx[0] = harmonic(hx_c[0], cond[0])
    lx[nx] = harmonic(cond[nx - 1], hx_c[1])
    for x in range(nx):
        here = cond[x]
        up = jnp.where(row == ny - 1, hy_rc[1, pl.ds(nx + x, 1), :], pltpu.roll(here, ny - 1, 0))
        ly[x] = harmonic(here, up)
        lylow[pl.ds(x, 1), :] = harmonic(hy_rc[0, pl.ds(nx + x, 1), :], here[0:1, :])
    apply(r, hx_r, lambda s, x: hy_rc[s, pl.ds(x, 1), :], z1)
    for s in (0, 1):
        for x in range(nx):
            py_z[s, pl.ds(x, 1), :] = z1[x, pl.ds(edge_y[s], 1), :]
    second = x_copies(z1, hx_z, 3) + y_copies(py_z, hy_z, 4)
    begin(second)
    mine[1:2, :] = sketch(z1)
    for s in (0, 1):
        recv_wait(hx_z, 3, s, z1.at[0], has_x[s], to_x[s])
        recv_wait(hy_z, 4, s, py_z.at[0], has_y[s], to_y[s])
    apply(z1, hx_z, lambda s, x: hy_z[s, pl.ds(x, 1), :], z2)
    mine[2:3, :] = sketch(z2)

    def share(step, carry):
        pltpu.make_async_remote_copy(
            src_ref=mine,
            dst_ref=gathered.at[me],
            send_sem=as_sem.at[step],
            recv_sem=ar_sem.at[me],
            device_id=peer(step),
            device_id_type=MESH,
        ).start()
        return carry

    lax.fori_loop(1, count, share, 0)
    gathered[me] = mine[...]
    arrive(first)
    arrive(second)

    def collect(step, carry):
        other = lax.rem(me + step, count)
        copy = pltpu.make_async_remote_copy(
            src_ref=mine,
            dst_ref=gathered.at[other],
            send_sem=as_sem.at[step],
            recv_sem=ar_sem.at[other],
            device_id=peer(step),
            device_id_type=MESH,
        )
        copy.wait_recv()
        copy.wait_send()
        return carry

    lax.fori_loop(1, count, collect, 0)
    summed = jnp.sum(gathered[...], axis=0)
    c0, c1 = coefficients(summed[0:1], summed[1:2], summed[2:3])
    for x in range(nx):
        answer[x] = c0 * r[x] + c1 * z1[x]
        rest[x] = r[x] - c0 * z1[x] - c1 * z2[x]


def body(ngx, ngy, f, w, m, s, d):
    nx, ny, nz = f.shape
    count = ngx * ngy
    vm = lambda shape, dtype=f32: pltpu.VMEM(shape, dtype)
    block = (nx, ny, nz)
    return pl.pallas_call(
        functools.partial(kernel, ngx, ngy, nx, ny, nz),
        out_shape=(vm(block), vm(block)),
        in_specs=[pl.BlockSpec(memory_space=pl.ANY)] * 5,
        out_specs=[pl.BlockSpec(memory_space=pltpu.VMEM)] * 2,
        scratch_shapes=[
            vm(block), vm(block),
            vm(block), vm(block), vm(block, jnp.int32), vm(block, jnp.int32), vm(block),
            vm(block), vm(block),
            vm((nx + 1, ny, nz)), vm(block), vm((nx, nz)), vm(block),
            vm((nx, ny, LOW, nz), bf16), vm(block), vm(block),
            vm((2, ny, nz)), vm((2, ny, nz)), vm((2, ny, nz)),
            vm((2, 2 * nx, nz)), vm((2, nx, nz)),
            vm((2, 2 * nx, nz)), vm((2, nx, nz)),
            vm((4, SKETCH)), vm((count, 4, SKETCH)),
            pltpu.SemaphoreType.DMA((5,)),
            pltpu.SemaphoreType.DMA((5, 2)),
            pltpu.SemaphoreType.DMA((5, 2)),
            pltpu.SemaphoreType.DMA((count,)),
            pltpu.SemaphoreType.DMA((count,)),
        ],
        compiler_params=pltpu.CompilerParams(collective_id=0, has_side_effects=True),
        name="sketched_gmres",
    )(f, w, m, s, d)


def solution(mesh):
    spec = P(("parts", "gx"), "gy", None)
    return jax.shard_map(
        functools.partial(body, mesh.shape["gx"], mesh.shape["gy"]),
        mesh=mesh,
        in_specs=(spec,) * 5,
        out_specs=(spec, spec),
        check_vma=False,
    )
```

```python
import functools

import jax
import jax.numpy as jnp
from jax import lax
from jax.experimental import pallas as pl
from jax.experimental.pallas import tpu as pltpu
from jax.sharding import PartitionSpec as P

SKETCH = 128
LOW = 16
HIGH = SKETCH // LOW
MESH = pl.DeviceIdType.MESH
epsilon = 1e-06
highest = lax.Precision.HIGHEST
f32 = jnp.float32
bf16 = jnp.bfloat16


def harmonic(first, second):
    return 2.0 * first * second / (first + second)


def total(field):
    return jnp.sum(jnp.sum(field, axis=1, keepdims=True), axis=0, keepdims=True)


def coefficients(s0, s1, s2):
    beta = jnp.sqrt(total(s0 * s0) + epsilon)
    inv_beta = 1.0 / beta
    q0 = s0 * inv_beta
    p0 = s1 * inv_beta
    h00 = total(q0 * p0)
    t0 = p0 - h00 * q0
    n0 = jnp.sqrt(total(t0 * t0) + epsilon)
    inv_n0 = 1.0 / n0
    q1 = t0 * inv_n0
    p1 = (s2 * inv_beta - h00 * p0) * inv_n0
    h01 = total(q0 * p1)
    h11 = total(q1 * p1)
    t1 = p1 - h01 * q0 - h11 * q1
    n1sq = total(t1 * t1) + epsilon
    m00 = h00 * h00 + n0 * n0
    m01 = h00 * h01 + n0 * h11
    m11 = h01 * h01 + h11 * h11 + n1sq
    b0 = beta * h00
    b1 = beta * h01
    l00 = jnp.sqrt(m00)
    l10 = m01 / l00
    l11 = jnp.sqrt(m11 - l10 * l10)
    f0 = b0 / l00
    f1 = (b1 - l10 * f0) / l11
    y1 = f1 / l11
    y0 = (f0 - l10 * y1) / l00
    c1 = y1 * inv_beta * inv_n0
    c0 = y0 * inv_beta - c1 * h00
    return c0, c1


def kernel(
    ngx, ngy, nx, ny, nz,
    f_hbm, w_hbm, m_hbm, s_hbm, d_hbm,
    answer, rest,
    z1, z2, r, w, m, slot, d, cond, cap, lx, ly, lylow, lz, onehot, wh, wl, rows,
    hx_r, hx_c, hx_z, hx_s, hx_d, hy_rc, hy_z, hy_s, hy_d, py_rc, py_z, py_s, py_d,
    mine, gathered, load_sem, hs_sem, hr_sem, as_sem, ar_sem,
):
    gx = lax.axis_index("gx")
    gy = lax.axis_index("gy")
    count = ngx * ngy
    me = gx * ngy + gy

    loads = [
        pltpu.make_async_copy(src, dst, load_sem.at[i])
        for i, (src, dst) in enumerate(
            ((w_hbm, w), (m_hbm, m), (f_hbm, r), (s_hbm, slot), (d_hbm, d))
        )
    ]
    for load in loads:
        load.start()

    def peer(step):
        other = lax.rem(me + step, count)
        return {"gx": lax.div(other, ngy), "gy": lax.rem(other, ngy)}

    barrier = pltpu.get_barrier_semaphore()

    def greet(step, carry):
        pl.semaphore_signal(barrier, inc=1, device_id=peer(step), device_id_type=MESH)
        return carry

    lax.fori_loop(1, count, greet, 0)

    has_x = (gx > 0, gx < ngx - 1)
    has_y = (gy > 0, gy < ngy - 1)
    to_x = ({"gx": gx - 1, "gy": gy}, {"gx": gx + 1, "gy": gy})
    to_y = ({"gx": gx, "gy": gy - 1}, {"gx": gx, "gy": gy + 1})
    edge_x = (0, nx - 1)
    edge_y = (0, ny - 1)

    def remote(src, dst, index, side, target):
        return pltpu.make_async_remote_copy(
            src_ref=src,
            dst_ref=dst.at[1 - side],
            send_sem=hs_sem.at[index, side],
            recv_sem=hr_sem.at[index, 1 - side],
            device_id=target,
            device_id_type=MESH,
        )

    def x_copies(src, dst, index):
        return [(has_x[s], remote(src.at[edge_x[s]], dst, index, s, to_x[s])) for s in (0, 1)]

    def y_copies(src, dst, index):
        return [(has_y[s], remote(src.at[s], dst, index, s, to_y[s])) for s in (0, 1)]

    def begin(copies):
        for there, copy in copies:
            pl.when(there)(copy.start)

    def arrive(copies):
        for there, copy in copies:
            pl.when(there)(copy.wait_send)

    def recv_wait(dst, index, side, src, there, target):
        copy = pltpu.make_async_remote_copy(
            src_ref=src,
            dst_ref=dst.at[side],
            send_sem=hs_sem.at[index, side],
            recv_sem=hr_sem.at[index, side],
            device_id=target,
            device_id_type=MESH,
        )
        pl.when(there)(copy.wait_recv)

    loads[0].wait()
    loads[1].wait()
    for x in range(nx):
        phase = m[x]
        cond[x] = jnp.where(phase == 0, 0.2, jnp.where(phase == 1, 1.0, 0.6)).astype(f32) * (0.5 + w[x])
        cap[x] = jnp.where(phase == 0, 1.0, jnp.where(phase == 1, 2.0, 1.5)).astype(f32)
    loads[2].wait()
    for s in (0, 1):
        for x in range(nx):
            py_rc[s, pl.ds(x, 1), :] = r[x, pl.ds(edge_y[s], 1), :]
            py_rc[s, pl.ds(nx + x, 1), :] = cond[x, pl.ds(edge_y[s], 1), :]

        @pl.when(jnp.logical_not(has_x[s]))
        def _():
            hx_r[s] = jnp.zeros((ny, nz), f32)
            hx_c[s] = jnp.zeros((ny, nz), f32)
            hx_z[s] = jnp.zeros((ny, nz), f32)
            hx_d[s] = jnp.zeros((ny, nz), f32)
            hx_s[s] = jnp.zeros((ny, nz), jnp.int32)

        @pl.when(jnp.logical_not(has_y[s]))
        def _():
            hy_rc[s] = jnp.zeros((2 * nx, nz), f32)
            hy_z[s] = jnp.zeros((nx, nz), f32)
            hy_d[s] = jnp.zeros((nx, nz), f32)
            hy_s[s] = jnp.zeros((nx, nz), jnp.int32)

    pl.semaphore_wait(barrier, count - 1)
    first = x_copies(cond, hx_c, 0) + y_copies(py_rc, hy_rc, 1) + x_copies(r, hx_r, 2)
    begin(first)
    loads[3].wait()
    loads[4].wait()
    for s in (0, 1):
        for x in range(nx):
            py_s[s, pl.ds(x, 1), :] = slot[x, pl.ds(edge_y[s], 1), :]
            py_d[s, pl.ds(x, 1), :] = d[x, pl.ds(edge_y[s], 1), :]
    for x in range(nx):
        rows[x] = slot[x]
    early = x_copies(slot, hx_s, 5) + y_copies(py_s, hy_s, 6) + x_copies(d, hx_d, 7) + y_copies(py_d, hy_d, 8)
    begin(early)

    lane = lax.broadcasted_iota(jnp.int32, (ny, nz), 1)
    row = lax.broadcasted_iota(jnp.int32, (ny, nz), 0)
    row_high = lax.broadcasted_iota(jnp.int32, (HIGH, nz), 0)
    row_low = lax.broadcasted_iota(jnp.int32, (LOW, nz), 0)

    def spread(x_ref, x, y, rows):
        return jnp.broadcast_to(x_ref[x, pl.ds(y, 1), :], (rows, nz))

    for x in range(nx):
        here = cond[x]
        if x > 0:
            lx[x] = harmonic(cond[x - 1], here)
        lz[x] = jnp.where(lane == nz - 1, 0.0, harmonic(here, pltpu.roll(here, nz - 1, 1)))

    def build(x, carry):
        for y in range(ny):
            slots = spread(rows, x, y, LOW)
            low = jnp.bitwise_and(slots, LOW - 1)
            onehot[x, y] = jnp.where(low == row_low, 1.0, 0.0).astype(bf16)
        return carry

    lax.fori_loop(0, nx, build, 0)

    def split(x, weighted):
        upper = weighted.astype(bf16).astype(f32)
        wh[x] = upper
        wl[x] = weighted - upper

    def sketch(planes, field):
        for x in range(nx):
            split(x, d[x] * field[x])

        def add(x, sums):
            for y in range(ny):
                mask = lax.shift_right_logical(spread(rows, x, y, HIGH), 4) == row_high
                left = jnp.concatenate(
                    [
                        jnp.where(mask, spread(wh, x, y, HIGH), 0.0),
                        jnp.where(mask, spread(wl, x, y, HIGH), 0.0),
                    ],
                    axis=0,
                ).astype(bf16)
                sums = sums + lax.dot_general(
                    left, onehot[x, y], (((1,), (1,)), ((), ())), preferred_element_type=f32
                )
            return sums

        sums = lax.fori_loop(0, planes, add, jnp.zeros((2 * HIGH, LOW), f32))
        both = sums[:HIGH] + sums[HIGH:]
        lanes = lax.broadcasted_iota(jnp.int32, (LOW, SKETCH), 1)
        expand = jnp.where(
            jnp.bitwise_and(lanes, LOW - 1) == lax.broadcasted_iota(jnp.int32, (LOW, SKETCH), 0), 1.0, 0.0
        ).astype(f32)
        wide = jnp.dot(both, expand, precision=highest, preferred_element_type=f32)
        keep = lax.shift_right_logical(
            lax.broadcasted_iota(jnp.int32, (HIGH, SKETCH), 1), 4
        ) == lax.broadcasted_iota(jnp.int32, (HIGH, SKETCH), 0)
        return jnp.sum(jnp.where(keep, wide, 0.0), axis=0, keepdims=True)

    def apply(field, halo_x, halo_y, out):
        for x in range(nx):
            v = field[x]
            if x == 0:
                low = v if halo_x is None else v - halo_x[0]
            else:
                low = v - field[x - 1]
            if x == nx - 1:
                top = v if halo_x is None else v - halo_x[1]
            else:
                top = v - field[x + 1]
            acc = cap[x] * v + lx[x + 1] * top + lx[x] * low
            first_row, last_row = (0.0, 0.0) if halo_y is None else (halo_y(0, x), halo_y(1, x))
            up = jnp.where(row == ny - 1, last_row, pltpu.roll(v, ny - 1, 0))
            flux = ly[x] * (v - up)
            entering = lylow[pl.ds(x, 1), :] * (first_row - v[0:1, :])
            acc = acc + flux - jnp.where(row == 0, entering, pltpu.roll(flux, 1, 0))
            flux = lz[x] * (v - pltpu.roll(v, nz - 1, 1))
            out[x] = acc + flux - pltpu.roll(flux, 1, 1)

    mine[3:4, :] = jnp.zeros((1, SKETCH), f32)
    mine[0:1, :] = sketch(nx, r)

    for s in (0, 1):
        recv_wait(hx_c, 0, s, cond.at[0], has_x[s], to_x[s])
        recv_wait(hy_rc, 1, s, py_rc.at[0], has_y[s], to_y[s])
        recv_wait(hx_r, 2, s, r.at[0], has_x[s], to_x[s])
    lx[0] = harmonic(hx_c[0], cond[0])
    lx[nx] = harmonic(cond[nx - 1], hx_c[1])
    for x in range(nx):
        here = cond[x]
        up = jnp.where(row == ny - 1, hy_rc[1, pl.ds(nx + x, 1), :], pltpu.roll(here, ny - 1, 0))
        ly[x] = harmonic(here, up)
        lylow[pl.ds(x, 1), :] = harmonic(hy_rc[0, pl.ds(nx + x, 1), :], here[0:1, :])
    apply(r, hx_r, lambda s, x: hy_rc[s, pl.ds(x, 1), :], z1)
    for s in (0, 1):
        for x in range(nx):
            py_z[s, pl.ds(x, 1), :] = z1[x, pl.ds(edge_y[s], 1), :]
    second = x_copies(z1, hx_z, 3) + y_copies(py_z, hy_z, 4)
    begin(second)
    mine[1:2, :] = sketch(nx, z1)
    for s in (0, 1):
        recv_wait(hx_s, 5, s, slot.at[0], has_x[s], to_x[s])
        recv_wait(hy_s, 6, s, py_s.at[0], has_y[s], to_y[s])
        recv_wait(hx_d, 7, s, d.at[0], has_x[s], to_x[s])
        recv_wait(hy_d, 8, s, py_d.at[0], has_y[s], to_y[s])
        rows[nx + s] = hx_s[s]
        split(nx + s, -lx[nx * s] * z1[edge_x[s]] * hx_d[s])
        edge = []
        for x in range(nx):
            link = lylow[pl.ds(x, 1), :] if s == 0 else ly[x, pl.ds(ny - 1, 1), :]
            edge.append(-link * z1[x, pl.ds(edge_y[s], 1), :] * hy_d[s, pl.ds(x, 1), :])
            rows[nx + 2, pl.ds(s * nx + x, 1), :] = hy_s[s, pl.ds(x, 1), :]
        edge = jnp.concatenate(edge, axis=0)
        upper = edge.astype(bf16).astype(f32)
        wh[nx + 2, pl.ds(s * nx, nx), :] = upper
        wl[nx + 2, pl.ds(s * nx, nx), :] = edge - upper
    for y in range(2 * nx, ny):
        rows[nx + 2, pl.ds(y, 1), :] = jnp.zeros((1, nz), jnp.int32)
        wh[nx + 2, pl.ds(y, 1), :] = jnp.zeros((1, nz), f32)
        wl[nx + 2, pl.ds(y, 1), :] = jnp.zeros((1, nz), f32)
    lax.fori_loop(nx, nx + 3, build, 0)
    apply(z1, None, None, z2)
    mine[2:3, :] = sketch(nx + 3, z2)

    def share(step, carry):
        pltpu.make_async_remote_copy(
            src_ref=mine,
            dst_ref=gathered.at[me],
            send_sem=as_sem.at[step],
            recv_sem=ar_sem.at[me],
            device_id=peer(step),
            device_id_type=MESH,
        ).start()
        return carry

    lax.fori_loop(1, count, share, 0)
    gathered[me] = mine[...]
    arrive(first)
    arrive(early)
    arrive(second)
    for s in (0, 1):
        recv_wait(hx_z, 3, s, z1.at[0], has_x[s], to_x[s])
        recv_wait(hy_z, 4, s, py_z.at[0], has_y[s], to_y[s])
        z2[edge_x[s]] = z2[edge_x[s]] - lx[nx * s] * hx_z[s]
        for x in range(nx):
            link = lylow[pl.ds(x, 1), :] if s == 0 else ly[x, pl.ds(ny - 1, 1), :]
            at = (x, pl.ds(edge_y[s], 1), slice(None))
            z2[at] = z2[at] - link * hy_z[s, pl.ds(x, 1), :]

    def collect(step, carry):
        other = lax.rem(me + step, count)
        copy = pltpu.make_async_remote_copy(
            src_ref=mine,
            dst_ref=gathered.at[other],
            send_sem=as_sem.at[step],
            recv_sem=ar_sem.at[other],
            device_id=peer(step),
            device_id_type=MESH,
        )
        copy.wait_recv()
        copy.wait_send()
        return carry

    lax.fori_loop(1, count, collect, 0)
    summed = jnp.sum(gathered[...], axis=0)
    c0, c1 = coefficients(summed[0:1], summed[1:2], summed[2:3])
    for x in range(nx):
        answer[x] = c0 * r[x] + c1 * z1[x]
        rest[x] = r[x] - c0 * z1[x] - c1 * z2[x]


def body(ngx, ngy, f, w, m, s, d):
    nx, ny, nz = f.shape
    count = ngx * ngy
    vm = lambda shape, dtype=f32: pltpu.VMEM(shape, dtype)
    block = (nx, ny, nz)
    wide = (nx + 3, ny, nz)
    assert 2 * nx <= ny
    return pl.pallas_call(
        functools.partial(kernel, ngx, ngy, nx, ny, nz),
        out_shape=(vm(block), vm(block)),
        in_specs=[pl.BlockSpec(memory_space=pl.ANY)] * 5,
        out_specs=[pl.BlockSpec(memory_space=pltpu.VMEM)] * 2,
        scratch_shapes=[
            vm(block), vm(block),
            vm(block), vm(block), vm(block, jnp.int32), vm(block, jnp.int32), vm(block),
            vm(block), vm(block),
            vm((nx + 1, ny, nz)), vm(block), vm((nx, nz)), vm(block),
            vm((nx + 3, ny, LOW, nz), bf16), vm(wide), vm(wide), vm(wide, jnp.int32),
            vm((2, ny, nz)), vm((2, ny, nz)), vm((2, ny, nz)), vm((2, ny, nz), jnp.int32), vm((2, ny, nz)),
            vm((2, 2 * nx, nz)), vm((2, nx, nz)), vm((2, nx, nz), jnp.int32), vm((2, nx, nz)),
            vm((2, 2 * nx, nz)), vm((2, nx, nz)), vm((2, nx, nz), jnp.int32), vm((2, nx, nz)),
            vm((4, SKETCH)), vm((count, 4, SKETCH)),
            pltpu.SemaphoreType.DMA((5,)),
            pltpu.SemaphoreType.DMA((9, 2)),
            pltpu.SemaphoreType.DMA((9, 2)),
            pltpu.SemaphoreType.DMA((count,)),
            pltpu.SemaphoreType.DMA((count,)),
        ],
        compiler_params=pltpu.CompilerParams(collective_id=0, has_side_effects=True),
        name="sketched_gmres",
    )(f, w, m, s, d)


def solution(mesh):
    spec = P(("parts", "gx"), "gy", None)
    return jax.shard_map(
        functools.partial(body, mesh.shape["gx"], mesh.shape["gy"]),
        mesh=mesh,
        in_specs=(spec,) * 5,
        out_specs=(spec, spec),
        check_vma=False,
    )
```

```python
import functools

import jax
import jax.numpy as jnp
from jax import lax
from jax.experimental import pallas as pl
from jax.experimental.pallas import tpu as pltpu
from jax.sharding import PartitionSpec as P

SKETCH = 128
LOW = 16
HIGH = SKETCH // LOW
MESH = pl.DeviceIdType.MESH
epsilon = 1e-06
highest = lax.Precision.HIGHEST
f32 = jnp.float32
bf16 = jnp.bfloat16


def harmonic(first, second):
    return 2.0 * first * second / (first + second)


def total(field):
    return jnp.sum(jnp.sum(field, axis=1, keepdims=True), axis=0, keepdims=True)


def coefficients(s0, s1, s2):
    beta = jnp.sqrt(total(s0 * s0) + epsilon)
    inv_beta = 1.0 / beta
    q0 = s0 * inv_beta
    p0 = s1 * inv_beta
    h00 = total(q0 * p0)
    t0 = p0 - h00 * q0
    n0 = jnp.sqrt(total(t0 * t0) + epsilon)
    inv_n0 = 1.0 / n0
    q1 = t0 * inv_n0
    p1 = (s2 * inv_beta - h00 * p0) * inv_n0
    h01 = total(q0 * p1)
    h11 = total(q1 * p1)
    t1 = p1 - h01 * q0 - h11 * q1
    n1sq = total(t1 * t1) + epsilon
    m00 = h00 * h00 + n0 * n0
    m01 = h00 * h01 + n0 * h11
    m11 = h01 * h01 + h11 * h11 + n1sq
    b0 = beta * h00
    b1 = beta * h01
    l00 = jnp.sqrt(m00)
    l10 = m01 / l00
    l11 = jnp.sqrt(m11 - l10 * l10)
    f0 = b0 / l00
    f1 = (b1 - l10 * f0) / l11
    y1 = f1 / l11
    y0 = (f0 - l10 * y1) / l00
    c1 = y1 * inv_beta * inv_n0
    c0 = y0 * inv_beta - c1 * h00
    return c0, c1


def kernel(
    ngx, ngy, nx, ny, nz,
    f_hbm, w_hbm, m_hbm, s_hbm, d_hbm,
    answer, rest,
    z1, z2, r, w, m, slot, d, cond, cap, lx, ly, lylow, lz, onehot, wh, wl, rows,
    hx_r, hx_c, hx_z, hx_s, hx_d, hy_rc, hy_z, hy_s, hy_d, py_rc, py_z, py_s, py_d,
    mine, gathered, load_sem, hs_sem, hr_sem, as_sem, ar_sem, known,
):
    gx = lax.axis_index("gx")
    gy = lax.axis_index("gy")
    count = ngx * ngy
    me = gx * ngy + gy

    loads = [
        pltpu.make_async_copy(src, dst, load_sem.at[i])
        for i, (src, dst) in enumerate(
            ((w_hbm, w), (m_hbm, m), (f_hbm, r), (s_hbm, slot), (d_hbm, d))
        )
    ]
    for load in loads:
        load.start()

    def peer(step):
        other = lax.rem(me + step, count)
        return {"gx": lax.div(other, ngy), "gy": lax.rem(other, ngy)}

    barrier = pltpu.get_barrier_semaphore()

    for step in range(1, ngx):
        other = {"gx": lax.rem(gx + step, ngx), "gy": gy}
        pl.semaphore_signal(barrier, inc=1, device_id=other, device_id_type=MESH)

    has_x = (gx > 0, gx < ngx - 1)
    has_y = (gy > 0, gy < ngy - 1)
    to_x = ({"gx": gx - 1, "gy": gy}, {"gx": gx + 1, "gy": gy})
    to_y = ({"gx": gx, "gy": gy - 1}, {"gx": gx, "gy": gy + 1})
    for s in (0, 1):

        @pl.when(has_y[s])
        def _():
            pl.semaphore_signal(barrier, inc=1, device_id=to_y[s], device_id_type=MESH)

    def tell(turn):
        for s in (0, 1):

            @pl.when(has_y[s])
            def _():
                pl.semaphore_signal(known.at[turn, 1 - s], inc=1, device_id=to_y[s], device_id_type=MESH)

    def hear(turn):
        for s in (0, 1):

            @pl.when(has_y[s])
            def _():
                pl.semaphore_wait(known.at[turn, s], 1)

    edge_x = (0, nx - 1)
    edge_y = (0, ny - 1)

    def remote(src, dst, index, side, target):
        return pltpu.make_async_remote_copy(
            src_ref=src,
            dst_ref=dst.at[1 - side],
            send_sem=hs_sem.at[index, side],
            recv_sem=hr_sem.at[index, 1 - side],
            device_id=target,
            device_id_type=MESH,
        )

    def x_copies(src, dst, index):
        return [(has_x[s], remote(src.at[edge_x[s]], dst, index, s, to_x[s])) for s in (0, 1)]

    def y_copies(src, dst, index):
        return [(has_y[s], remote(src.at[s], dst, index, s, to_y[s])) for s in (0, 1)]

    def begin(copies):
        for there, copy in copies:
            pl.when(there)(copy.start)

    def arrive(copies):
        for there, copy in copies:
            pl.when(there)(copy.wait_send)

    def recv_wait(dst, index, side, src, there, target):
        copy = pltpu.make_async_remote_copy(
            src_ref=src,
            dst_ref=dst.at[side],
            send_sem=hs_sem.at[index, side],
            recv_sem=hr_sem.at[index, side],
            device_id=target,
            device_id_type=MESH,
        )
        pl.when(there)(copy.wait_recv)

    loads[0].wait()
    loads[1].wait()
    for x in range(nx):
        phase = m[x]
        cond[x] = jnp.where(phase == 0, 0.2, jnp.where(phase == 1, 1.0, 0.6)).astype(f32) * (0.5 + w[x])
        cap[x] = jnp.where(phase == 0, 1.0, jnp.where(phase == 1, 2.0, 1.5)).astype(f32)
    loads[2].wait()
    for s in (0, 1):
        for x in range(nx):
            py_rc[s, pl.ds(x, 1), :] = r[x, pl.ds(edge_y[s], 1), :]
            py_rc[s, pl.ds(nx + x, 1), :] = cond[x, pl.ds(edge_y[s], 1), :]

        @pl.when(jnp.logical_not(has_x[s]))
        def _():
            hx_r[s] = jnp.zeros((ny, nz), f32)
            hx_c[s] = jnp.zeros((ny, nz), f32)
            hx_z[s] = jnp.zeros((ny, nz), f32)
            hx_d[s] = jnp.zeros((ny, nz), f32)
            hx_s[s] = jnp.zeros((ny, nz), jnp.int32)

        @pl.when(jnp.logical_not(has_y[s]))
        def _():
            hy_rc[s] = jnp.zeros((2 * nx, nz), f32)
            hy_z[s] = jnp.zeros((nx, nz), f32)
            hy_d[s] = jnp.zeros((nx, nz), f32)
            hy_s[s] = jnp.zeros((nx, nz), jnp.int32)

    pl.semaphore_wait(barrier, ngx - 1 + has_y[0].astype(jnp.int32) + has_y[1].astype(jnp.int32))
    first = x_copies(cond, hx_c, 0) + y_copies(py_rc, hy_rc, 1) + x_copies(r, hx_r, 2)
    begin(first)
    loads[3].wait()
    loads[4].wait()
    for s in (0, 1):
        for x in range(nx):
            py_s[s, pl.ds(x, 1), :] = slot[x, pl.ds(edge_y[s], 1), :]
            py_d[s, pl.ds(x, 1), :] = d[x, pl.ds(edge_y[s], 1), :]
    for x in range(nx):
        rows[x] = slot[x]
    early = x_copies(slot, hx_s, 5) + y_copies(py_s, hy_s, 6) + x_copies(d, hx_d, 7) + y_copies(py_d, hy_d, 8)
    begin(early)
    if ngy > 1:
        tell(1)

    lane = lax.broadcasted_iota(jnp.int32, (ny, nz), 1)
    row = lax.broadcasted_iota(jnp.int32, (ny, nz), 0)
    row_high = lax.broadcasted_iota(jnp.int32, (HIGH, nz), 0)
    row_low = lax.broadcasted_iota(jnp.int32, (LOW, nz), 0)

    def spread(x_ref, x, y, rows):
        return jnp.broadcast_to(x_ref[x, pl.ds(y, 1), :], (rows, nz))

    for x in range(nx):
        here = cond[x]
        if x > 0:
            lx[x] = harmonic(cond[x - 1], here)
        lz[x] = jnp.where(lane == nz - 1, 0.0, harmonic(here, pltpu.roll(here, nz - 1, 1)))

    def build(x, carry):
        for y in range(ny):
            slots = spread(rows, x, y, LOW)
            low = jnp.bitwise_and(slots, LOW - 1)
            onehot[x, y] = jnp.where(low == row_low, 1.0, 0.0).astype(bf16)
        return carry

    lax.fori_loop(0, nx, build, 0)

    def split(x, weighted):
        upper = weighted.astype(bf16).astype(f32)
        wh[x] = upper
        wl[x] = weighted - upper

    def sketch(planes, field):
        for x in range(nx):
            split(x, d[x] * field[x])

        def add(x, sums):
            for y in range(ny):
                mask = lax.shift_right_logical(spread(rows, x, y, HIGH), 4) == row_high
                left = jnp.concatenate(
                    [
                        jnp.where(mask, spread(wh, x, y, HIGH), 0.0),
                        jnp.where(mask, spread(wl, x, y, HIGH), 0.0),
                    ],
                    axis=0,
                ).astype(bf16)
                sums = sums + lax.dot_general(
                    left, onehot[x, y], (((1,), (1,)), ((), ())), preferred_element_type=f32
                )
            return sums

        sums = lax.fori_loop(0, planes, add, jnp.zeros((2 * HIGH, LOW), f32))
        both = sums[:HIGH] + sums[HIGH:]
        lanes = lax.broadcasted_iota(jnp.int32, (LOW, SKETCH), 1)
        expand = jnp.where(
            jnp.bitwise_and(lanes, LOW - 1) == lax.broadcasted_iota(jnp.int32, (LOW, SKETCH), 0), 1.0, 0.0
        ).astype(f32)
        wide = jnp.dot(both, expand, precision=highest, preferred_element_type=f32)
        keep = lax.shift_right_logical(
            lax.broadcasted_iota(jnp.int32, (HIGH, SKETCH), 1), 4
        ) == lax.broadcasted_iota(jnp.int32, (HIGH, SKETCH), 0)
        return jnp.sum(jnp.where(keep, wide, 0.0), axis=0, keepdims=True)

    def apply(field, halo_x, halo_y, out):
        for x in range(nx):
            v = field[x]
            if x == 0:
                low = v if halo_x is None else v - halo_x[0]
            else:
                low = v - field[x - 1]
            if x == nx - 1:
                top = v if halo_x is None else v - halo_x[1]
            else:
                top = v - field[x + 1]
            acc = cap[x] * v + lx[x + 1] * top + lx[x] * low
            first_row, last_row = (0.0, 0.0) if halo_y is None else (halo_y(0, x), halo_y(1, x))
            up = jnp.where(row == ny - 1, last_row, pltpu.roll(v, ny - 1, 0))
            flux = ly[x] * (v - up)
            entering = lylow[pl.ds(x, 1), :] * (first_row - v[0:1, :])
            acc = acc + flux - jnp.where(row == 0, entering, pltpu.roll(flux, 1, 0))
            flux = lz[x] * (v - pltpu.roll(v, nz - 1, 1))
            out[x] = acc + flux - pltpu.roll(flux, 1, 1)

    mine[3:4, :] = jnp.zeros((1, SKETCH), f32)
    mine[0:1, :] = sketch(nx, r)
    if ngy > 2:
        hear(1)
        tell(2)

    for s in (0, 1):
        recv_wait(hx_c, 0, s, cond.at[0], has_x[s], to_x[s])
        recv_wait(hy_rc, 1, s, py_rc.at[0], has_y[s], to_y[s])
        recv_wait(hx_r, 2, s, r.at[0], has_x[s], to_x[s])
    lx[0] = harmonic(hx_c[0], cond[0])
    lx[nx] = harmonic(cond[nx - 1], hx_c[1])
    for x in range(nx):
        here = cond[x]
        up = jnp.where(row == ny - 1, hy_rc[1, pl.ds(nx + x, 1), :], pltpu.roll(here, ny - 1, 0))
        ly[x] = harmonic(here, up)
        lylow[pl.ds(x, 1), :] = harmonic(hy_rc[0, pl.ds(nx + x, 1), :], here[0:1, :])
    apply(r, hx_r, lambda s, x: hy_rc[s, pl.ds(x, 1), :], z1)
    for s in (0, 1):
        for x in range(nx):
            py_z[s, pl.ds(x, 1), :] = z1[x, pl.ds(edge_y[s], 1), :]
    second = x_copies(z1, hx_z, 3) + y_copies(py_z, hy_z, 4)
    begin(second)
    for turn in range(3, ngy):
        hear(turn - 1)
        tell(turn)
    mine[1:2, :] = sketch(nx, z1)
    for s in (0, 1):
        recv_wait(hx_s, 5, s, slot.at[0], has_x[s], to_x[s])
        recv_wait(hy_s, 6, s, py_s.at[0], has_y[s], to_y[s])
        recv_wait(hx_d, 7, s, d.at[0], has_x[s], to_x[s])
        recv_wait(hy_d, 8, s, py_d.at[0], has_y[s], to_y[s])
        rows[nx + s] = hx_s[s]
        split(nx + s, -lx[nx * s] * z1[edge_x[s]] * hx_d[s])
        edge = []
        for x in range(nx):
            link = lylow[pl.ds(x, 1), :] if s == 0 else ly[x, pl.ds(ny - 1, 1), :]
            edge.append(-link * z1[x, pl.ds(edge_y[s], 1), :] * hy_d[s, pl.ds(x, 1), :])
            rows[nx + 2, pl.ds(s * nx + x, 1), :] = hy_s[s, pl.ds(x, 1), :]
        edge = jnp.concatenate(edge, axis=0)
        upper = edge.astype(bf16).astype(f32)
        wh[nx + 2, pl.ds(s * nx, nx), :] = upper
        wl[nx + 2, pl.ds(s * nx, nx), :] = edge - upper
    for y in range(2 * nx, ny):
        rows[nx + 2, pl.ds(y, 1), :] = jnp.zeros((1, nz), jnp.int32)
        wh[nx + 2, pl.ds(y, 1), :] = jnp.zeros((1, nz), f32)
        wl[nx + 2, pl.ds(y, 1), :] = jnp.zeros((1, nz), f32)
    lax.fori_loop(nx, nx + 3, build, 0)
    apply(z1, None, None, z2)
    mine[2:3, :] = sketch(nx + 3, z2)

    def share(step, carry):
        pltpu.make_async_remote_copy(
            src_ref=mine,
            dst_ref=gathered.at[me],
            send_sem=as_sem.at[step],
            recv_sem=ar_sem.at[me],
            device_id=peer(step),
            device_id_type=MESH,
        ).start()
        return carry

    if ngy > 1:
        hear(ngy - 1)
    lax.fori_loop(1, count, share, 0)
    gathered[me] = mine[...]
    arrive(first)
    arrive(early)
    arrive(second)
    for s in (0, 1):
        recv_wait(hx_z, 3, s, z1.at[0], has_x[s], to_x[s])
        recv_wait(hy_z, 4, s, py_z.at[0], has_y[s], to_y[s])
        z2[edge_x[s]] = z2[edge_x[s]] - lx[nx * s] * hx_z[s]
        for x in range(nx):
            link = lylow[pl.ds(x, 1), :] if s == 0 else ly[x, pl.ds(ny - 1, 1), :]
            at = (x, pl.ds(edge_y[s], 1), slice(None))
            z2[at] = z2[at] - link * hy_z[s, pl.ds(x, 1), :]

    def collect(step, carry):
        other = lax.rem(me + step, count)
        copy = pltpu.make_async_remote_copy(
            src_ref=mine,
            dst_ref=gathered.at[other],
            send_sem=as_sem.at[step],
            recv_sem=ar_sem.at[other],
            device_id=peer(step),
            device_id_type=MESH,
        )
        copy.wait_recv()
        copy.wait_send()
        return carry

    lax.fori_loop(1, count, collect, 0)
    summed = jnp.sum(gathered[...], axis=0)
    c0, c1 = coefficients(summed[0:1], summed[1:2], summed[2:3])
    for x in range(nx):
        answer[x] = c0 * r[x] + c1 * z1[x]
        rest[x] = r[x] - c0 * z1[x] - c1 * z2[x]


def put_out(answer, rest, answer_out, rest_out, sem):
    one = pltpu.make_async_copy(answer, answer_out, sem.at[0])
    two = pltpu.make_async_copy(rest, rest_out, sem.at[1])
    one.start()
    two.start()
    one.wait()
    two.wait()


def body(ngx, ngy, f, w, m, s, d):
    nx, ny, nz = f.shape
    count = ngx * ngy
    vm = lambda shape, dtype=f32: pltpu.VMEM(shape, dtype)
    block = (nx, ny, nz)
    wide = (nx + 3, ny, nz)
    assert 2 * nx <= ny
    answer, rest = pl.pallas_call(
        functools.partial(kernel, ngx, ngy, nx, ny, nz),
        out_shape=(vm(block), vm(block)),
        in_specs=[pl.BlockSpec(memory_space=pl.ANY)] * 5,
        out_specs=[pl.BlockSpec(memory_space=pltpu.VMEM)] * 2,
        scratch_shapes=[
            vm(block), vm(block),
            vm(block), vm(block), vm(block, jnp.int32), vm(block, jnp.int32), vm(block),
            vm(block), vm(block),
            vm((nx + 1, ny, nz)), vm(block), vm((nx, nz)), vm(block),
            vm((nx + 3, ny, LOW, nz), bf16), vm(wide), vm(wide), vm(wide, jnp.int32),
            vm((2, ny, nz)), vm((2, ny, nz)), vm((2, ny, nz)), vm((2, ny, nz), jnp.int32), vm((2, ny, nz)),
            vm((2, 2 * nx, nz)), vm((2, nx, nz)), vm((2, nx, nz), jnp.int32), vm((2, nx, nz)),
            vm((2, 2 * nx, nz)), vm((2, nx, nz)), vm((2, nx, nz), jnp.int32), vm((2, nx, nz)),
            vm((4, SKETCH)), vm((count, 4, SKETCH)),
            pltpu.SemaphoreType.DMA((5,)),
            pltpu.SemaphoreType.DMA((9, 2)),
            pltpu.SemaphoreType.DMA((9, 2)),
            pltpu.SemaphoreType.DMA((count,)),
            pltpu.SemaphoreType.DMA((count,)),
            pltpu.SemaphoreType.REGULAR((ngy, 2)),
        ],
        compiler_params=pltpu.CompilerParams(collective_id=0, has_side_effects=True),
        name="sketched_gmres",
    )(f, w, m, s, d)
    return pl.pallas_call(
        put_out,
        out_shape=(jax.ShapeDtypeStruct(block, f32), jax.ShapeDtypeStruct(block, f32)),
        in_specs=[pl.BlockSpec(memory_space=pltpu.VMEM)] * 2,
        out_specs=[pl.BlockSpec(memory_space=pl.ANY)] * 2,
        scratch_shapes=[pltpu.SemaphoreType.DMA((2,))],
        name="put_out",
    )(pltpu.with_memory_space_constraint(answer, pltpu.VMEM), pltpu.with_memory_space_constraint(rest, pltpu.VMEM))


def solution(mesh):
    spec = P(("parts", "gx"), "gy", None)
    return jax.shard_map(
        functools.partial(body, mesh.shape["gx"], mesh.shape["gy"]),
        mesh=mesh,
        in_specs=(spec,) * 5,
        out_specs=(spec, spec),
        check_vma=False,
    )
```

```python
import functools

import jax
import jax.numpy as jnp
from jax import lax
from jax.experimental import pallas as pl
from jax.experimental.pallas import tpu as pltpu
from jax.sharding import PartitionSpec as P

SKETCH = 128
LOW = 16
HIGH = SKETCH // LOW
MESH = pl.DeviceIdType.MESH
epsilon = 1e-06
highest = lax.Precision.HIGHEST
f32 = jnp.float32
bf16 = jnp.bfloat16


def harmonic(first, second):
    return 2.0 * first * second / (first + second)


def total(field):
    return jnp.sum(jnp.sum(field, axis=1, keepdims=True), axis=0, keepdims=True)


def coefficients(s0, s1, s2):
    beta = jnp.sqrt(total(s0 * s0) + epsilon)
    inv_beta = 1.0 / beta
    q0 = s0 * inv_beta
    p0 = s1 * inv_beta
    h00 = total(q0 * p0)
    t0 = p0 - h00 * q0
    n0 = jnp.sqrt(total(t0 * t0) + epsilon)
    inv_n0 = 1.0 / n0
    q1 = t0 * inv_n0
    p1 = (s2 * inv_beta - h00 * p0) * inv_n0
    h01 = total(q0 * p1)
    h11 = total(q1 * p1)
    t1 = p1 - h01 * q0 - h11 * q1
    n1sq = total(t1 * t1) + epsilon
    m00 = h00 * h00 + n0 * n0
    m01 = h00 * h01 + n0 * h11
    m11 = h01 * h01 + h11 * h11 + n1sq
    b0 = beta * h00
    b1 = beta * h01
    l00 = jnp.sqrt(m00)
    l10 = m01 / l00
    l11 = jnp.sqrt(m11 - l10 * l10)
    f0 = b0 / l00
    f1 = (b1 - l10 * f0) / l11
    y1 = f1 / l11
    y0 = (f0 - l10 * y1) / l00
    c1 = y1 * inv_beta * inv_n0
    c0 = y0 * inv_beta - c1 * h00
    return c0, c1


def kernel(
    ngx, ngy, nx, ny, nz,
    f_hbm, w_hbm, m_hbm, s_hbm, d_hbm,
    answer, rest,
    z1, z2, r, w, m, slot, d, cond, cap, lx, ly, lylow, lz, onehot, wh, wl, wh1, wl1, rows,
    hx_r, hx_c, hx_z, hx_s, hx_d, hy_rc, hy_z, hy_s, hy_d, py_rc, py_z, py_s, py_d,
    mine, gathered, load_sem, hs_sem, hr_sem, as_sem, ar_sem, known,
):
    gx = lax.axis_index("gx")
    gy = lax.axis_index("gy")
    count = ngx * ngy
    me = gx * ngy + gy

    loads = [
        pltpu.make_async_copy(src, dst, load_sem.at[i])
        for i, (src, dst) in enumerate(
            ((w_hbm, w), (m_hbm, m), (f_hbm, r), (s_hbm, slot), (d_hbm, d))
        )
    ]
    for load in loads:
        load.start()

    def peer(step):
        other = lax.rem(me + step, count)
        return {"gx": lax.div(other, ngy), "gy": lax.rem(other, ngy)}

    barrier = pltpu.get_barrier_semaphore()

    for step in range(1, ngx):
        other = {"gx": lax.rem(gx + step, ngx), "gy": gy}
        pl.semaphore_signal(barrier, inc=1, device_id=other, device_id_type=MESH)

    has_x = (gx > 0, gx < ngx - 1)
    has_y = (gy > 0, gy < ngy - 1)
    to_x = ({"gx": gx - 1, "gy": gy}, {"gx": gx + 1, "gy": gy})
    to_y = ({"gx": gx, "gy": gy - 1}, {"gx": gx, "gy": gy + 1})
    for s in (0, 1):

        @pl.when(has_y[s])
        def _():
            pl.semaphore_signal(barrier, inc=1, device_id=to_y[s], device_id_type=MESH)

    def tell(turn):
        for s in (0, 1):

            @pl.when(has_y[s])
            def _():
                pl.semaphore_signal(known.at[turn, 1 - s], inc=1, device_id=to_y[s], device_id_type=MESH)

    def hear(turn):
        for s in (0, 1):

            @pl.when(has_y[s])
            def _():
                pl.semaphore_wait(known.at[turn, s], 1)

    edge_x = (0, nx - 1)
    edge_y = (0, ny - 1)

    def remote(src, dst, index, side, target):
        return pltpu.make_async_remote_copy(
            src_ref=src,
            dst_ref=dst.at[1 - side],
            send_sem=hs_sem.at[index, side],
            recv_sem=hr_sem.at[index, 1 - side],
            device_id=target,
            device_id_type=MESH,
        )

    def x_copies(src, dst, index):
        return [(has_x[s], remote(src.at[edge_x[s]], dst, index, s, to_x[s])) for s in (0, 1)]

    def y_copies(src, dst, index):
        return [(has_y[s], remote(src.at[s], dst, index, s, to_y[s])) for s in (0, 1)]

    def begin(copies):
        for there, copy in copies:
            pl.when(there)(copy.start)

    def arrive(copies):
        for there, copy in copies:
            pl.when(there)(copy.wait_send)

    def recv_wait(dst, index, side, src, there, target):
        copy = pltpu.make_async_remote_copy(
            src_ref=src,
            dst_ref=dst.at[side],
            send_sem=hs_sem.at[index, side],
            recv_sem=hr_sem.at[index, side],
            device_id=target,
            device_id_type=MESH,
        )
        pl.when(there)(copy.wait_recv)

    loads[0].wait()
    loads[1].wait()
    for x in range(nx):
        phase = m[x]
        cond[x] = jnp.where(phase == 0, 0.2, jnp.where(phase == 1, 1.0, 0.6)).astype(f32) * (0.5 + w[x])
        cap[x] = jnp.where(phase == 0, 1.0, jnp.where(phase == 1, 2.0, 1.5)).astype(f32)
    loads[2].wait()
    for s in (0, 1):
        for x in range(nx):
            py_rc[s, pl.ds(x, 1), :] = r[x, pl.ds(edge_y[s], 1), :]
            py_rc[s, pl.ds(nx + x, 1), :] = cond[x, pl.ds(edge_y[s], 1), :]

        @pl.when(jnp.logical_not(has_x[s]))
        def _():
            hx_r[s] = jnp.zeros((ny, nz), f32)
            hx_c[s] = jnp.zeros((ny, nz), f32)
            hx_z[s] = jnp.zeros((ny, nz), f32)
            hx_d[s] = jnp.zeros((ny, nz), f32)
            hx_s[s] = jnp.zeros((ny, nz), jnp.int32)

        @pl.when(jnp.logical_not(has_y[s]))
        def _():
            hy_rc[s] = jnp.zeros((2 * nx, nz), f32)
            hy_z[s] = jnp.zeros((nx, nz), f32)
            hy_d[s] = jnp.zeros((nx, nz), f32)
            hy_s[s] = jnp.zeros((nx, nz), jnp.int32)

    pl.semaphore_wait(barrier, ngx - 1 + has_y[0].astype(jnp.int32) + has_y[1].astype(jnp.int32))
    first = x_copies(cond, hx_c, 0) + y_copies(py_rc, hy_rc, 1) + x_copies(r, hx_r, 2)
    begin(first)
    loads[3].wait()
    loads[4].wait()
    for s in (0, 1):
        for x in range(nx):
            py_s[s, pl.ds(x, 1), :] = slot[x, pl.ds(edge_y[s], 1), :]
            py_d[s, pl.ds(x, 1), :] = d[x, pl.ds(edge_y[s], 1), :]
    for x in range(nx):
        rows[x] = slot[x]
    early = x_copies(slot, hx_s, 5) + y_copies(py_s, hy_s, 6) + x_copies(d, hx_d, 7) + y_copies(py_d, hy_d, 8)
    begin(early)
    if ngy > 1:
        tell(1)

    lane = lax.broadcasted_iota(jnp.int32, (ny, nz), 1)
    row = lax.broadcasted_iota(jnp.int32, (ny, nz), 0)
    row_high = lax.broadcasted_iota(jnp.int32, (HIGH, nz), 0)
    row_low = lax.broadcasted_iota(jnp.int32, (LOW, nz), 0)

    def spread(x_ref, x, y, rows):
        return jnp.broadcast_to(x_ref[x, pl.ds(y, 1), :], (rows, nz))

    for x in range(nx):
        here = cond[x]
        if x > 0:
            lx[x] = harmonic(cond[x - 1], here)
        lz[x] = jnp.where(lane == nz - 1, 0.0, harmonic(here, pltpu.roll(here, nz - 1, 1)))

    def build(x, carry):
        for y in range(ny):
            slots = spread(rows, x, y, LOW)
            low = jnp.bitwise_and(slots, LOW - 1)
            onehot[x, y] = jnp.where(low == row_low, 1.0, 0.0).astype(bf16)
        return carry

    lax.fori_loop(0, nx, build, 0)

    def split(x, weighted):
        upper = weighted.astype(bf16).astype(f32)
        wh[x] = upper
        wl[x] = weighted - upper

    def adder(parts):
        def add(x, sums):
            for y in range(ny):
                mask = lax.shift_right_logical(spread(rows, x, y, HIGH), 4) == row_high
                left = jnp.concatenate(
                    [jnp.where(mask, spread(part, x, y, HIGH), 0.0) for part in parts], axis=0
                ).astype(bf16)
                sums = sums + lax.dot_general(
                    left, onehot[x, y], (((1,), (1,)), ((), ())), preferred_element_type=f32
                )
            return sums

        return add

    def finish(sums):
        both = sums[:HIGH] + sums[HIGH:]
        lanes = lax.broadcasted_iota(jnp.int32, (LOW, SKETCH), 1)
        expand = jnp.where(
            jnp.bitwise_and(lanes, LOW - 1) == lax.broadcasted_iota(jnp.int32, (LOW, SKETCH), 0), 1.0, 0.0
        ).astype(f32)
        wide = jnp.dot(both, expand, precision=highest, preferred_element_type=f32)
        keep = lax.shift_right_logical(
            lax.broadcasted_iota(jnp.int32, (HIGH, SKETCH), 1), 4
        ) == lax.broadcasted_iota(jnp.int32, (HIGH, SKETCH), 0)
        return jnp.sum(jnp.where(keep, wide, 0.0), axis=0, keepdims=True)

    def apply(field, halo_x, halo_y, out):
        for x in range(nx):
            v = field[x]
            if x == 0:
                low = v if halo_x is None else v - halo_x[0]
            else:
                low = v - field[x - 1]
            if x == nx - 1:
                top = v if halo_x is None else v - halo_x[1]
            else:
                top = v - field[x + 1]
            acc = cap[x] * v + lx[x + 1] * top + lx[x] * low
            first_row, last_row = (0.0, 0.0) if halo_y is None else (halo_y(0, x), halo_y(1, x))
            up = jnp.where(row == ny - 1, last_row, pltpu.roll(v, ny - 1, 0))
            flux = ly[x] * (v - up)
            entering = lylow[pl.ds(x, 1), :] * (first_row - v[0:1, :])
            acc = acc + flux - jnp.where(row == 0, entering, pltpu.roll(flux, 1, 0))
            flux = lz[x] * (v - pltpu.roll(v, nz - 1, 1))
            out[x] = acc + flux - pltpu.roll(flux, 1, 1)

    mine[3:4, :] = jnp.zeros((1, SKETCH), f32)
    for x in range(nx):
        split(x, d[x] * r[x])
    mine[0:1, :] = finish(lax.fori_loop(0, nx, adder((wh, wl)), jnp.zeros((2 * HIGH, LOW), f32)))
    if ngy > 2:
        hear(1)
        tell(2)

    for s in (0, 1):
        recv_wait(hx_c, 0, s, cond.at[0], has_x[s], to_x[s])
        recv_wait(hy_rc, 1, s, py_rc.at[0], has_y[s], to_y[s])
        recv_wait(hx_r, 2, s, r.at[0], has_x[s], to_x[s])
    lx[0] = harmonic(hx_c[0], cond[0])
    lx[nx] = harmonic(cond[nx - 1], hx_c[1])
    for x in range(nx):
        here = cond[x]
        up = jnp.where(row == ny - 1, hy_rc[1, pl.ds(nx + x, 1), :], pltpu.roll(here, ny - 1, 0))
        ly[x] = harmonic(here, up)
        lylow[pl.ds(x, 1), :] = harmonic(hy_rc[0, pl.ds(nx + x, 1), :], here[0:1, :])
    apply(r, hx_r, lambda s, x: hy_rc[s, pl.ds(x, 1), :], z1)
    for s in (0, 1):
        for x in range(nx):
            py_z[s, pl.ds(x, 1), :] = z1[x, pl.ds(edge_y[s], 1), :]
    second = x_copies(z1, hx_z, 3) + y_copies(py_z, hy_z, 4)
    begin(second)
    for turn in range(3, ngy):
        hear(turn - 1)
        tell(turn)
    apply(z1, None, None, z2)
    for x in range(nx):
        weighted = d[x] * z1[x]
        upper = weighted.astype(bf16).astype(f32)
        wh1[x] = upper
        wl1[x] = weighted - upper
        split(x, d[x] * z2[x])
    sums = lax.fori_loop(0, nx, adder((wh1, wl1, wh, wl)), jnp.zeros((4 * HIGH, LOW), f32))
    for s in (0, 1):
        recv_wait(hx_s, 5, s, slot.at[0], has_x[s], to_x[s])
        recv_wait(hy_s, 6, s, py_s.at[0], has_y[s], to_y[s])
        recv_wait(hx_d, 7, s, d.at[0], has_x[s], to_x[s])
        recv_wait(hy_d, 8, s, py_d.at[0], has_y[s], to_y[s])
        rows[nx + s] = hx_s[s]
        split(nx + s, -lx[nx * s] * z1[edge_x[s]] * hx_d[s])
        edge = []
        for x in range(nx):
            link = lylow[pl.ds(x, 1), :] if s == 0 else ly[x, pl.ds(ny - 1, 1), :]
            edge.append(-link * z1[x, pl.ds(edge_y[s], 1), :] * hy_d[s, pl.ds(x, 1), :])
            rows[nx + 2, pl.ds(s * nx + x, 1), :] = hy_s[s, pl.ds(x, 1), :]
        edge = jnp.concatenate(edge, axis=0)
        upper = edge.astype(bf16).astype(f32)
        wh[nx + 2, pl.ds(s * nx, nx), :] = upper
        wl[nx + 2, pl.ds(s * nx, nx), :] = edge - upper
    for y in range(2 * nx, ny):
        rows[nx + 2, pl.ds(y, 1), :] = jnp.zeros((1, nz), jnp.int32)
        wh[nx + 2, pl.ds(y, 1), :] = jnp.zeros((1, nz), f32)
        wl[nx + 2, pl.ds(y, 1), :] = jnp.zeros((1, nz), f32)
    lax.fori_loop(nx, nx + 3, build, 0)
    halo_sums = lax.fori_loop(nx, nx + 3, adder((wh, wl)), jnp.zeros((2 * HIGH, LOW), f32))
    mine[1:2, :] = finish(sums[: 2 * HIGH])
    mine[2:3, :] = finish(sums[2 * HIGH :] + halo_sums)

    def share(step, carry):
        pltpu.make_async_remote_copy(
            src_ref=mine,
            dst_ref=gathered.at[me],
            send_sem=as_sem.at[step],
            recv_sem=ar_sem.at[me],
            device_id=peer(step),
            device_id_type=MESH,
        ).start()
        return carry

    if ngy > 1:
        hear(ngy - 1)
    lax.fori_loop(1, count, share, 0)
    gathered[me] = mine[...]
    arrive(first)
    arrive(early)
    arrive(second)
    for s in (0, 1):
        recv_wait(hx_z, 3, s, z1.at[0], has_x[s], to_x[s])
        recv_wait(hy_z, 4, s, py_z.at[0], has_y[s], to_y[s])
        z2[edge_x[s]] = z2[edge_x[s]] - lx[nx * s] * hx_z[s]
        for x in range(nx):
            link = lylow[pl.ds(x, 1), :] if s == 0 else ly[x, pl.ds(ny - 1, 1), :]
            at = (x, pl.ds(edge_y[s], 1), slice(None))
            z2[at] = z2[at] - link * hy_z[s, pl.ds(x, 1), :]

    def collect(step, carry):
        other = lax.rem(me + step, count)
        copy = pltpu.make_async_remote_copy(
            src_ref=mine,
            dst_ref=gathered.at[other],
            send_sem=as_sem.at[step],
            recv_sem=ar_sem.at[other],
            device_id=peer(step),
            device_id_type=MESH,
        )
        copy.wait_recv()
        copy.wait_send()
        return carry

    lax.fori_loop(1, count, collect, 0)
    summed = jnp.sum(gathered[...], axis=0)
    c0, c1 = coefficients(summed[0:1], summed[1:2], summed[2:3])
    for x in range(nx):
        answer[x] = c0 * r[x] + c1 * z1[x]
        rest[x] = r[x] - c0 * z1[x] - c1 * z2[x]


def put_out(answer, rest, answer_out, rest_out, sem):
    one = pltpu.make_async_copy(answer, answer_out, sem.at[0])
    two = pltpu.make_async_copy(rest, rest_out, sem.at[1])
    one.start()
    two.start()
    one.wait()
    two.wait()


def body(ngx, ngy, f, w, m, s, d):
    nx, ny, nz = f.shape
    count = ngx * ngy
    vm = lambda shape, dtype=f32: pltpu.VMEM(shape, dtype)
    block = (nx, ny, nz)
    wide = (nx + 3, ny, nz)
    assert 2 * nx <= ny
    answer, rest = pl.pallas_call(
        functools.partial(kernel, ngx, ngy, nx, ny, nz),
        out_shape=(vm(block), vm(block)),
        in_specs=[pl.BlockSpec(memory_space=pl.ANY)] * 5,
        out_specs=[pl.BlockSpec(memory_space=pltpu.VMEM)] * 2,
        scratch_shapes=[
            vm(block), vm(block),
            vm(block), vm(block), vm(block, jnp.int32), vm(block, jnp.int32), vm(block),
            vm(block), vm(block),
            vm((nx + 1, ny, nz)), vm(block), vm((nx, nz)), vm(block),
            vm((nx + 3, ny, LOW, nz), bf16), vm(wide), vm(wide), vm(block), vm(block), vm(wide, jnp.int32),
            vm((2, ny, nz)), vm((2, ny, nz)), vm((2, ny, nz)), vm((2, ny, nz), jnp.int32), vm((2, ny, nz)),
            vm((2, 2 * nx, nz)), vm((2, nx, nz)), vm((2, nx, nz), jnp.int32), vm((2, nx, nz)),
            vm((2, 2 * nx, nz)), vm((2, nx, nz)), vm((2, nx, nz), jnp.int32), vm((2, nx, nz)),
            vm((4, SKETCH)), vm((count, 4, SKETCH)),
            pltpu.SemaphoreType.DMA((5,)),
            pltpu.SemaphoreType.DMA((9, 2)),
            pltpu.SemaphoreType.DMA((9, 2)),
            pltpu.SemaphoreType.DMA((count,)),
            pltpu.SemaphoreType.DMA((count,)),
            pltpu.SemaphoreType.REGULAR((ngy, 2)),
        ],
        compiler_params=pltpu.CompilerParams(collective_id=0, has_side_effects=True),
        name="sketched_gmres",
    )(f, w, m, s, d)
    return pl.pallas_call(
        put_out,
        out_shape=(jax.ShapeDtypeStruct(block, f32), jax.ShapeDtypeStruct(block, f32)),
        in_specs=[pl.BlockSpec(memory_space=pltpu.VMEM)] * 2,
        out_specs=[pl.BlockSpec(memory_space=pl.ANY)] * 2,
        scratch_shapes=[pltpu.SemaphoreType.DMA((2,))],
        name="put_out",
    )(pltpu.with_memory_space_constraint(answer, pltpu.VMEM), pltpu.with_memory_space_constraint(rest, pltpu.VMEM))


def solution(mesh):
    spec = P(("parts", "gx"), "gy", None)
    return jax.shard_map(
        functools.partial(body, mesh.shape["gx"], mesh.shape["gy"]),
        mesh=mesh,
        in_specs=(spec,) * 5,
        out_specs=(spec, spec),
        check_vma=False,
    )
```
